32 devices in a mesh: gx: 2 (over y), gy: 4 (over z), gz: 4 (over x, core).
Axes of the slice: x: 2, y: 2, z: 4, core: 2. Of those that a mesh axis runs over, the one named last changes fastest.
Arguments:
- load_cases: float32 [2, 128, 32, 256], P(None, 'gz', 'gy', 'gx'), may hold values from -6 to 6
- density_level: int32 [128, 32, 256], P('gz', 'gy', 'gx'), may hold values from 0 to 7
Outputs:
- solution: float32 [2, 128, 32, 256], P(None, 'gz', 'gy', 'gx')
The draws below stay inside these ranges and needn't reach their ends.
All inputs are finite; a program needn't handle non-finite values.
Results may differ from the reference program's by a relative error of at most 0.00011.
Values sent between devices are 32-bit elements; how exact they have to be, the bound alone decides.
A program may use at most 192 MiB of HBM per device.

```python
import math
import jax
import jax.numpy as jnp

CASES = 2
LEVELS = 8
NX = 256
NY = 32
NZ = 128


def draw_load_cases(key, part):
    full_shape = (CASES, NZ, NY, NX)
    return jnp.clip(jax.random.normal(key, full_shape, jnp.float32), -6.0, 6.0)


def plant(result, key, least, high):
    place = [jax.random.randint(jax.random.fold_in(key, axis), (), 0, length) for axis, length in enumerate(result.shape)]
    longest = result.shape.index(max(result.shape))
    neighbour = place[:longest] + [(place[longest] + 1) % result.shape[longest]] + place[longest + 1:]
    return result.at[tuple(place)].set(least).at[tuple(neighbour)].set(high)


def setup_inputs(seed: int = 0) -> dict:
    key_list = jax.random.split(jax.random.key(seed), 3)
    return {
        "load_cases": draw_load_cases(jax.random.fold_in(key_list[2], 71), 0),
        "density_level": plant(jax.random.randint(key_list[1], (NZ, NY, NX), 0, LEVELS), jax.random.fold_in(key_list[1], 1), 0, LEVELS - 1).astype(jnp.int32),
    }


middle_point = 0.646875
half_range = 0.503125
first_weight = 1.0 / (middle_point + half_range * math.cos(math.pi / 4))
second_weight = 1.0 / (middle_point - half_range * math.cos(math.pi / 4))


def smooth_sum(padded):
    padded = 0.5 * padded[:, :-2] + padded[:, 1:-1] + 0.5 * padded[:, 2:]
    padded = 0.5 * padded[:, :, :-2] + padded[:, :, 1:-1] + 0.5 * padded[:, :, 2:]
    return 0.5 * padded[..., :-2] + padded[..., 1:-1] + 0.5 * padded[..., 2:]


def operate(values, stiffness, spacing_sq):
    padded = jnp.pad(values, ((0, 0), (1, 1), (1, 1), (1, 1)))
    return stiffness * (16.0 * values - 2.0 * smooth_sum(padded)) / spacing_sq


def jacobi(residue, stiffness, spacing_sq):
    return residue * (spacing_sq / (14.0 * stiffness))


def restrict(values):
    return values.reshape(values.shape[0], values.shape[1] // 2, 2, values.shape[2] // 2, 2, values.shape[3] // 2, 2).mean(axis=(2, 4, 6))


def prolong(values):
    return jnp.repeat(jnp.repeat(jnp.repeat(values, 2, axis=1), 2, axis=2), 2, axis=3)


def presmooth(target, stiffness, spacing_sq):
    guess = first_weight * jacobi(target, stiffness, spacing_sq)
    return guess + second_weight * jacobi(target - operate(guess, stiffness, spacing_sq), stiffness, spacing_sq)


def postsmooth(guess, target, stiffness, spacing_sq):
    guess = guess + first_weight * jacobi(target - operate(guess, stiffness, spacing_sq), stiffness, spacing_sq)
    return guess + second_weight * jacobi(target - operate(guess, stiffness, spacing_sq), stiffness, spacing_sq)


def reference(load_cases, density_level):
    stiffness_fine = (0.05 + 0.95 * (density_level.astype(jnp.float32) / (LEVELS - 1)) ** 3)[None]
    guess_fine = presmooth(load_cases, stiffness_fine, 1.0)
    rhs_mid = restrict(load_cases - operate(guess_fine, stiffness_fine, 1.0))
    stiffness_mid = restrict(stiffness_fine)
    guess_mid = presmooth(rhs_mid, stiffness_mid, 4.0)
    rhs_low = restrict(rhs_mid - operate(guess_mid, stiffness_mid, 4.0))
    stiffness_low = restrict(stiffness_mid)
    guess_low = presmooth(rhs_low, stiffness_low, 16.0)
    rhs_base = restrict(rhs_low - operate(guess_low, stiffness_low, 16.0))
    stiffness_base = restrict(stiffness_low)
    guess_base = postsmooth(presmooth(rhs_base, stiffness_base, 64.0), rhs_base, stiffness_base, 64.0)
    guess_low = postsmooth(guess_low + prolong(guess_base), rhs_low, stiffness_low, 16.0)
    guess_mid = postsmooth(guess_mid + prolong(guess_low), rhs_mid, stiffness_mid, 4.0)
    return postsmooth(guess_fine + prolong(guess_mid), load_cases, stiffness_fine, 1.0)
```

```python
import math

import jax
import jax.numpy as jnp
from jax import lax
from jax.sharding import PartitionSpec as P

LEVELS = 8
middle_point = 0.646875
half_range = 0.503125
first_weight = 1.0 / (middle_point + half_range * math.cos(math.pi / 4))
second_weight = 1.0 / (middle_point - half_range * math.cos(math.pi / 4))
SIDES = (("gy", 2), ("gz", 1), ("gx", 3))


def with_halo(cells, width):
    for axis, dim in SIDES:
        count = lax.axis_size(axis)
        ends = count - 1
        head = lax.slice_in_dim(cells, 0, width, axis=dim)
        tail = lax.slice_in_dim(cells, cells.shape[dim] - width, cells.shape[dim], axis=dim)
        cells = jnp.concatenate(
            [
                lax.ppermute(tail, axis, [(i, i + 1) for i in range(ends)]),
                cells,
                lax.ppermute(head, axis, [(i + 1, i) for i in range(ends)]),
            ],
            axis=dim,
        )
    return cells


def crop(values, width):
    if width == 0:
        return values
    return values[:, width:-width, width:-width, width:-width]


def smooth_sum(padded):
    padded = 0.5 * (padded[:, :-2] + padded[:, 2:]) + padded[:, 1:-1]
    padded = 0.5 * (padded[:, :, :-2] + padded[:, :, 2:]) + padded[:, :, 1:-1]
    return 0.5 * (padded[..., :-2] + padded[..., 2:]) + padded[..., 1:-1]


def residue(padded, target, stiffness, spacing_sq):
    return target - stiffness * (16.0 * crop(padded, 1) - 2.0 * smooth_sum(padded)) * (1.0 / spacing_sq)


def step(padded, target, stiffness, inverse, weight, spacing_sq):
    return crop(padded, 1) + weight * inverse * residue(padded, target, stiffness, spacing_sq)


def invert(stiffness, spacing_sq):
    inside = stiffness > 0.0
    return jnp.where(inside, spacing_sq / (14.0 * jnp.where(inside, stiffness, 1.0)), 0.0)


def restrict(values):
    return values.reshape(
        values.shape[0], values.shape[1] // 2, 2, values.shape[2] // 2, 2, values.shape[3] // 2, 2
    ).mean(axis=(2, 4, 6))


def prolong(values):
    return jnp.repeat(jnp.repeat(jnp.repeat(values, 2, axis=1), 2, axis=2), 2, axis=3)


def pad(values, width=1):
    return jnp.pad(values, ((0, 0),) + ((width, width),) * 3)


def post(guess, target, stiffness, inverse, spacing_sq):
    guess = step(pad(guess), target, stiffness, inverse, first_weight, spacing_sq)
    return step(pad(guess), target, stiffness, inverse, second_weight, spacing_sq)


def pre(target, stiffness, inverse, spacing_sq):
    guess = first_weight * inverse * target
    return step(pad(guess), target, stiffness, inverse, second_weight, spacing_sq)


def coarse_cycle(rhs, stiffness):
    inverse = invert(stiffness, 16.0)
    guess = pre(rhs, stiffness, inverse, 16.0)
    rhs_base = restrict(residue(pad(guess), rhs, stiffness, 16.0))
    stiffness_base = restrict(stiffness)
    inverse_base = invert(stiffness_base, 64.0)
    guess_base = pre(rhs_base, stiffness_base, inverse_base, 64.0)
    guess_base = post(guess_base, rhs_base, stiffness_base, inverse_base, 64.0)
    return post(guess + prolong(guess_base), rhs, stiffness, inverse, 16.0)


def gather_all(block):
    counts = [lax.axis_size(axis) for axis in ("gz", "gy", "gx")]
    fields, z, y, x = block.shape
    whole = lax.all_gather(block, ("gz", "gy", "gx"), axis=0, tiled=False)
    whole = whole.reshape(*counts, fields, z, y, x).transpose(3, 0, 4, 1, 5, 2, 6)
    return whole.reshape(fields, counts[0] * z, counts[1] * y, counts[2] * x)


def body(load_cases, density_level):
    stiffness_own = (0.05 + 0.95 * (density_level.astype(jnp.float32) / (LEVELS - 1)) ** 3)[None]
    stiffness_mid_own = restrict(stiffness_own)
    stiffness_low = restrict(stiffness_mid_own)

    fine = with_halo(jnp.concatenate([load_cases, stiffness_own], axis=0), 3)
    target, stiffness = fine[:2], fine[2:]
    inverse = invert(stiffness, 1.0)
    guess_fine = step(
        first_weight * inverse * target, crop(target, 1), crop(stiffness, 1), crop(inverse, 1), second_weight, 1.0
    )
    rhs_mid_own = restrict(residue(crop(guess_fine, 1), load_cases, stiffness_own, 1.0))

    mid = with_halo(jnp.concatenate([rhs_mid_own, stiffness_mid_own], axis=0), 4)
    rhs_mid, stiffness_mid = mid[:2], mid[2:]
    inverse_mid = invert(stiffness_mid, 4.0)
    guess_mid = step(
        first_weight * inverse_mid * rhs_mid,
        crop(rhs_mid, 1), crop(stiffness_mid, 1), crop(inverse_mid, 1), second_weight, 4.0,
    )
    rhs_low = restrict(residue(crop(guess_mid, 2), rhs_mid_own, stiffness_mid_own, 4.0))

    own = rhs_low.shape
    low = gather_all(jnp.concatenate([rhs_low, stiffness_low], axis=0))
    guess_low = pad(coarse_cycle(low[:2], low[2:]), 2)
    starts = [0] + [lax.axis_index(axis) * size for axis, size in zip(("gz", "gy", "gx"), own[1:])]
    guess_low = lax.dynamic_slice(guess_low, starts, (own[0],) + tuple(size + 4 for size in own[1:]))

    guess_mid = guess_mid + crop(prolong(guess_low), 1)
    guess_mid = step(
        guess_mid, crop(rhs_mid, 2), crop(stiffness_mid, 2), crop(inverse_mid, 2), first_weight, 4.0
    )
    guess_mid = step(
        guess_mid, crop(rhs_mid, 3), crop(stiffness_mid, 3), crop(inverse_mid, 3), second_weight, 4.0
    )

    guess_fine = guess_fine + prolong(guess_mid)
    guess_fine = step(
        guess_fine, crop(target, 2), crop(stiffness, 2), crop(inverse, 2), first_weight, 1.0
    )
    return step(guess_fine, load_cases, stiffness_own, crop(inverse, 3), second_weight, 1.0)


def solution(mesh):
    in_specs = (P(None, "gz", "gy", "gx"), P("gz", "gy", "gx"))
    out_specs = P(None, "gz", "gy", "gx")
    return jax.shard_map(body, mesh=mesh, in_specs=in_specs, out_specs=out_specs, check_vma=False)
```
